32 devices in a mesh: row: 8 (over z, y), col: 4 (over x, core).
Axes of the slice: x: 2, y: 2, z: 4, core: 2. Of those that a mesh axis runs over, the one named last changes fastest.
Arguments:
- hidden_act: bfloat16 [768, 26624], P('col', 'row'), may hold values from -6 to 6
- out_grad: bfloat16 [768, 16384], P('row', 'col'), may hold values from -6 to 6
- down_weight: bfloat16 [26624, 16384], P('row', 'col'), may hold values from -0.046875 to 0.046875
Outputs:
- fisher: float32 [26624, 16384], P('row', 'col')
- hidden_grad: bfloat16 [768, 26624], P('col', 'row')
The draws below stay inside these ranges and needn't reach their ends.
All inputs are finite; a program needn't handle non-finite values.
Results may differ from the reference program's by a relative error of at most 0.001.
Values may be sent and summed in bfloat16 or wider, within the bound.
No kernel may reach another device: no remote copies, remote signals or barrier semaphores. Data moves between devices by JAX's collectives and lax.ppermute only.
A program may use at most 192 MiB of HBM per device.

```python
import jax
import jax.numpy as jnp
from jax import lax

D = 16384
FFW = 26624
SEQ = 96
EXAMPLES = 8
TOKENS = 768


def spiked(result, rng, source, target, parts, factor):
    owner, partner = [(jnp.arange(result.shape[dim]) // (result.shape[dim] // parts)).reshape([-1 if axis == dim else 1 for axis in range(result.ndim)]) for dim in (source, target)]
    chosen = jax.random.permutation(rng, parts)[partner]
    strong = (owner == chosen) | (owner == (partner + parts // 2) % parts)
    return jnp.where(strong, factor * result, result)


def block_levels(own_key, shape, pieces, smallest, top_value):
    gain, own = 1.0, jax.random.fold_in(own_key, 6)
    for position, parts in pieces:
        draws = jnp.exp(jax.random.uniform(jax.random.fold_in(own, position), (parts,), jnp.float32, smallest / len(pieces), top_value / len(pieces)))
        gain = gain * jnp.repeat(draws, shape[position] // parts).reshape([-1 if axis == position else 1 for axis in range(len(shape))])
    return gain


def gaussian(own_key, shape, width, reach, split=(), kind=jnp.bfloat16):
    drawn = jax.random.normal(own_key, shape, jnp.float32) * width
    if len(split) > 0:
        drawn = block_levels(own_key, shape, split, -0.22, 0.18) * drawn
    return jnp.clip(drawn, min=-reach, max=reach).astype(kind)


def gaussian_with(stream_key, extent, scale, reach, pieces, heavy, dtype=jnp.bfloat16):
    drawn = scale * jax.random.normal(stream_key, extent, jnp.float32)
    if pieces:
        drawn = drawn * block_levels(stream_key, extent, pieces, -0.22, 0.18)
    return jnp.clip(spiked(drawn, jax.random.fold_in(stream_key, 3), *heavy), -reach, reach).astype(dtype)


def setup_inputs(seed: int = 0) -> dict:
    keys = jax.random.split(jax.random.key(seed), 4)
    hidden_act = gaussian(keys[0], (TOKENS, FFW), 1.0, 6.0, ((0, 4), (1, 8)))
    out_grad = gaussian_with(keys[1], (TOKENS, D), 1.0, 6.0, ((0, 8), (1, 4)), (1, 0, 8, 2.0))
    down_weight = gaussian(keys[2], (FFW, D), D ** -0.5, 0.046875, ((0, 8), (1, 4)))
    return dict(hidden_act=hidden_act, out_grad=out_grad, down_weight=down_weight)


def reference(hidden_act, out_grad, down_weight):
    acts = hidden_act.reshape(EXAMPLES, SEQ, FFW)
    grads = out_grad.reshape(EXAMPLES, SEQ, D)

    def step(total, pair):
        grad_e = lax.dot_general(pair[0], pair[1], (((0,), (0,)), ((), ())), preferred_element_type=jnp.float32)
        return total + grad_e * grad_e, None

    total, unused = lax.scan(step, jnp.zeros((FFW, D), jnp.float32), (acts, grads))
    fisher = total / (EXAMPLES * SEQ)
    hidden_grad = lax.dot_general(out_grad, down_weight, (((1,), (1,)), ((), ())), preferred_element_type=jnp.float32)
    return fisher, hidden_grad.astype(jnp.bfloat16)
```

```python
import functools

import jax
import jax.numpy as jnp
from jax import lax
from jax.experimental import pallas as pl
from jax.experimental.pallas import tpu as pltpu
from jax.sharding import PartitionSpec as P

SEQ = 96
EXAMPLES = 8
LANES = 128


def largest_block(size, limit):
    return max(b for b in range(LANES, limit + 1, LANES) if size % b == 0)


def fisher_kernel(act_ref, grad_ref, out_ref, rows_ref, *, width):
    depth = rows_ref.shape[1] // EXAMPLES
    columns = out_ref.shape[1]

    for e in range(EXAMPLES):
        piece = act_ref[e * SEQ : (e + 1) * SEQ, :]
        rows_ref[:, e * depth : e * depth + SEQ] = piece.T

    for j in range(0, columns, width):
        total = None
        for e in range(EXAMPLES):
            grad_e = lax.dot_general(
                rows_ref[:, e * depth : e * depth + SEQ],
                grad_ref[e * SEQ : (e + 1) * SEQ, j : j + width],
                (((1,), (0,)), ((), ())),
                preferred_element_type=jnp.float32,
            )
            total = grad_e * grad_e if total is None else total + grad_e * grad_e
        out_ref[:, j : j + width] = total * (1.0 / (EXAMPLES * SEQ))


def fisher_of(act, grad):
    tokens, rows = act.shape
    columns = grad.shape[1]
    block = largest_block(rows, 256)
    width = largest_block(columns, 256)
    return pl.pallas_call(
        functools.partial(fisher_kernel, width=width),
        out_shape=jax.ShapeDtypeStruct((rows, columns), jnp.float32),
        grid=(rows // block,),
        in_specs=[
            pl.BlockSpec((tokens, block), lambda i: (0, i)),
            pl.BlockSpec((tokens, columns), lambda i: (0, 0), pipeline_mode=pl.Buffered(1)),
        ],
        out_specs=pl.BlockSpec((block, columns), lambda i: (i, 0)),
        scratch_shapes=[pltpu.VMEM((block, EXAMPLES * LANES), act.dtype)],
        cost_estimate=pl.CostEstimate(
            flops=2 * tokens * rows * columns,
            bytes_accessed=4 * rows * columns + 2 * tokens * (rows + columns),
            transcendentals=0,
        ),
        compiler_params=pltpu.CompilerParams(dimension_semantics=("arbitrary",)),
        name="fisher",
    )(act, grad)


def per_device(hidden_act, out_grad, down_weight):
    grad_whole = lax.all_gather(out_grad, "row", axis=0, tiled=True)
    act_whole = lax.all_gather(hidden_act, "col", axis=0, tiled=True)
    summed = lax.psum_scatter(
        lax.dot_general(
            grad_whole, down_weight, (((1,), (1,)), ((), ())), preferred_element_type=jnp.float32
        ),
        "col",
        scatter_dimension=0,
        tiled=True,
    )
    return (fisher_of(act_whole, grad_whole), summed.astype(jnp.bfloat16))


def solution(mesh):
    placed = (P("col", "row"), P("row", "col"), P("row", "col"))
    return jax.shard_map(
        per_device,
        mesh=mesh,
        in_specs=placed,
        out_specs=(P("row", "col"), P("col", "row")),
        check_vma=False,
    )
```

```python
import functools

import jax
import jax.numpy as jnp
import numpy as np
from jax import lax
from jax.experimental import pallas as pl
from jax.experimental.pallas import tpu as pltpu
from jax.sharding import PartitionSpec as P


SEQ = 96
EXAMPLES = 8
LANES = 128
EIGHTHS = (3, 5)
SPLITS = 3
BUFFERS = 4
POWER_TOP = 2.0**7.75

F32 = jnp.float32
ROWS_BY_ROWS = (((1,), (1,)), ((), ()))
ROWS_BY_COLUMNS = (((1,), (0,)), ((), ()))


def largest_block(size, limit):
    return max(b for b in range(LANES, limit + 1, LANES) if size % b == 0)


def params(mib=None):
    limit = {} if mib is None else {"vmem_limit_bytes": mib << 20}
    return pltpu.CompilerParams(dimension_semantics=("arbitrary",), **limit)


def in_vmem():
    return pl.BlockSpec(memory_space=pltpu.VMEM)


def turn_kernel(*refs, slot, step):
    act_refs, rows_ref = refs[:2], refs[-1]
    for act_ref in act_refs:
        for row in range(0, act_ref.shape[0], SEQ):
            for units in range(0, act_ref.shape[1], step):
                rows_ref[slot, units : units + step, :SEQ] = act_ref[
                    row : row + SEQ, units : units + step
                ].T
            slot += 1


def turned(acts, held, slot):
    units = acts[0].shape[1]
    return pl.pallas_call(
        functools.partial(turn_kernel, slot=slot, step=largest_block(units, 256)),
        out_shape=jax.ShapeDtypeStruct((EXAMPLES, units, LANES), acts[0].dtype),
        in_specs=[in_vmem()] * (2 + len(held)),
        out_specs=in_vmem(),
        input_output_aliases={2: 0} if held else {},
        cost_estimate=pl.CostEstimate(
            flops=4 * acts[0].size, bytes_accessed=8 * acts[0].size, transcendentals=0
        ),
        compiler_params=pltpu.CompilerParams(vmem_limit_bytes=16 << 20),
    )(*acts, *held)


def fisher_kernel(at_ref, rows_ref, *refs, width, part, block, first, blocks, start):
    grad_refs = refs[:EXAMPLES]
    fisher_ref, out_ref, sems = refs[-3:]
    parts = grad_refs[0].shape[1] // part

    def units(i):
        return pl.ds(pl.multiple_of((first + i) * block, block), block)

    def sending(i, n):
        return pltpu.make_async_copy(
            out_ref.at[n], fisher_ref.at[units(i), pl.ds(start + n * part, part)], sems.at[n]
        )

    def one_block(i, carry):
        for n in range(parts):

            @pl.when(i > 0)
            def _():
                sending(i - 1, n).wait()

            for j in range(0, part, width):
                total = None
                for s, grad_ref in enumerate(grad_refs):
                    grad_e = lax.dot_general(
                        rows_ref[at_ref[s], units(i), :SEQ],
                        grad_ref[:, n * part + j : n * part + j + width],
                        ROWS_BY_COLUMNS,
                        preferred_element_type=F32,
                    )
                    total = grad_e * grad_e if total is None else total + grad_e * grad_e
                out_ref[n, :, j : j + width] = total * (1.0 / (EXAMPLES * SEQ))
            sending(i, n).start()
        return carry

    lax.fori_loop(0, blocks, one_block, 0)
    for n in range(parts):
        sending(blocks - 1, n).wait()


def row_block(units):
    return max(b for b in range(16, 417, 16) if units % b == 0)


def fisher_part(at, rows, grads, held, shape, first, blocks, start):
    block = row_block(shape[0])
    columns = grads[0].shape[1]
    part = largest_block(columns, columns // 2)
    in_specs = [pl.BlockSpec(memory_space=pltpu.SMEM)] + [in_vmem()] * (1 + len(grads))
    operands = [at, rows, *grads]
    aliases = {}
    if held is not None:
        aliases = {len(operands): 0}
        operands.append(held)
        in_specs.append(pl.BlockSpec(memory_space=pl.ANY))
    tokens = EXAMPLES * SEQ
    return pl.pallas_call(
        functools.partial(
            fisher_kernel,
            width=largest_block(part, 256),
            part=part,
            block=block,
            first=first,
            blocks=blocks,
            start=start,
        ),
        out_shape=jax.ShapeDtypeStruct(shape, F32),
        in_specs=in_specs,
        out_specs=pl.BlockSpec(memory_space=pl.ANY),
        scratch_shapes=[
            pltpu.VMEM((columns // part, block, part), F32),
            pltpu.SemaphoreType.DMA((columns // part,)),
        ],
        input_output_aliases=aliases,
        cost_estimate=pl.CostEstimate(
            flops=5 * tokens * blocks * block * columns,
            bytes_accessed=4 * blocks * block * columns,
            transcendentals=0,
        ),
        compiler_params=pltpu.CompilerParams(vmem_limit_bytes=16 << 20),
    )(*operands)


def hidden_kernel(to_ref, *refs, places, block, start):
    grad_refs, weight_ref = refs[:EXAMPLES], refs[EXAMPLES]
    held_refs, out_refs = refs[EXAMPLES + 1 : -3 - places], refs[-3 - places : -3]
    tokens_ref, buffer_ref, sems = refs[-3:]
    columns = grad_refs[0].shape[1]
    blocks = weight_ref.shape[0] // block

    def units(i):
        return pl.ds(pl.multiple_of(i * block, block), block)

    def fetching(i):
        slot = lax.rem(i, BUFFERS)
        return pltpu.make_async_copy(
            weight_ref.at[units(i), pl.ds(start, columns)], buffer_ref.at[slot], sems.at[slot]
        )

    for i in range(min(BUFFERS - 1, blocks)):
        fetching(jnp.int32(i)).start()
    for s in range(EXAMPLES):
        tokens_ref[to_ref[s]] = grad_refs[s][...]

    def one_block(i, carry):
        @pl.when(i + BUFFERS - 1 < blocks)
        def _():
            fetching(i + BUFFERS - 1).start()

        fetching(i).wait()
        tokens = tokens_ref[...].reshape(EXAMPLES * SEQ, columns)
        part = lax.dot_general(
            tokens, buffer_ref[lax.rem(i, BUFFERS)], ROWS_BY_ROWS, preferred_element_type=F32
        )
        rows = part.shape[0] // places
        for n, out_ref in enumerate(out_refs):
            piece = part[n * rows : (n + 1) * rows]
            out_ref[:, units(i)] = piece + held_refs[n][:, units(i)] if held_refs else piece
        return carry

    lax.fori_loop(0, blocks, one_block, 0)


def hidden_part(to, grads, weight, held, places, start):
    units = weight.shape[0]
    columns = grads[0].shape[1]
    block = largest_block(units, 256)
    rows = EXAMPLES * SEQ // places
    return pl.pallas_call(
        functools.partial(hidden_kernel, places=places, block=block, start=start),
        out_shape=[jax.ShapeDtypeStruct((rows, units), F32)] * places,
        in_specs=[pl.BlockSpec(memory_space=pltpu.SMEM)]
        + [in_vmem()] * EXAMPLES
        + [pl.BlockSpec(memory_space=pl.ANY)]
        + [in_vmem()] * len(held),
        out_specs=[in_vmem()] * places,
        scratch_shapes=[
            pltpu.VMEM((EXAMPLES, SEQ, columns), weight.dtype),
            pltpu.VMEM((BUFFERS, block, columns), weight.dtype),
            pltpu.SemaphoreType.DMA((BUFFERS,)),
        ],
        input_output_aliases={2 + EXAMPLES + n: n for n in range(len(held))},
        cost_estimate=pl.CostEstimate(
            flops=2 * EXAMPLES * SEQ * units * columns,
            bytes_accessed=2 * units * columns,
            transcendentals=0,
        ),
        compiler_params=pltpu.CompilerParams(vmem_limit_bytes=28 << 20),
    )(to, *grads, weight, *held)


def encode_kernel(a_ref, b_ref, code_ref):
    total = a_ref[...] + b_ref[...]
    units = total.shape[1]
    top = jnp.maximum(jnp.max(jnp.abs(total), axis=1, keepdims=True), 1e-35) * 1.004
    scale = jnp.broadcast_to(top, (total.shape[0], LANES)).astype(code_ref.dtype)
    code_ref[:, units:] = scale
    share = total * (POWER_TOP / scale.astype(F32)[:, :1])
    power = share * share
    power = power * power
    power = power * power
    power = power * power
    code_ref[:, :units] = jnp.where(share < 0, -power, power).astype(code_ref.dtype)


def decode_kernel(*refs):
    mine_ref, other_ref, code_refs, out_ref = refs[0], refs[1], refs[2:-1], refs[-1]
    total = mine_ref[...] + other_ref[...]
    units = total.shape[1]
    for code_ref in code_refs:
        power = code_ref[:, :units].astype(F32)
        root = jnp.exp(jnp.log(jnp.abs(power)) * (1.0 / 16))
        scale = code_ref[:, units:].astype(F32)[:, :1] * (1.0 / POWER_TOP)
        total = total + jnp.where(power < 0, -root, root) * scale
    out_ref[...] = total.astype(out_ref.dtype)


def by_rows(kernel, out_columns, dtype, *arrays):
    rows = arrays[0].shape[0]
    block = 48 if rows % 48 == 0 else rows
    return pl.pallas_call(
        kernel,
        out_shape=jax.ShapeDtypeStruct((rows, out_columns), dtype),
        grid=(rows // block,),
        in_specs=[pl.BlockSpec((block, a.shape[1]), lambda i: (i, 0)) for a in arrays],
        out_specs=pl.BlockSpec((block, out_columns), lambda i: (i, 0)),
        cost_estimate=pl.CostEstimate(
            flops=10 * rows * out_columns, bytes_accessed=8 * rows * out_columns, transcendentals=0
        ),
        compiler_params=params(20),
    )(*arrays)


def ring_places(size):
    return list(range(0, size, 2)) + list(range(size - 1, 0, -2))


def ring_gather(piece, size):
    ring = ring_places(size)
    right = [(ring[n], ring[(n + 1) % size]) for n in range(size)]
    left = [(b, a) for a, b in right]
    found, from_left, from_right = [piece], piece, piece
    for step in range(1, size // 2 + 1):
        from_left = lax.ppermute(from_left, "row", right)
        found.append(from_left)
        if step < size - size // 2:
            from_right = lax.ppermute(from_right, "row", left)
            found.append(from_right)
    return found


def ring_rows(size):
    steps = [0]
    for step in range(1, size // 2 + 1):
        steps.append(size - step)
        if step < size - size // 2:
            steps.append(step)
    row = lax.axis_index("row").astype(jnp.uint32)
    mine = jnp.where(row % 2 == 0, row // 2, size - 1 - row // 2)
    places = (mine + np.array(steps, np.uint32)) % size
    return jnp.where(places < size // 2, 2 * places, 2 * (size - 1 - places) + 1)


def pipelined(hidden_act, out_grad, down_weight, row_size, col_size):
    chips = col_size // 2
    units, features = down_weight.shape
    per_col = hidden_act.shape[0] // SEQ
    other_core = [(c, c ^ 1) for c in range(col_size)]
    ahead = {
        d: [(c, (c + 2 * d) % col_size) for c in range(col_size)] for d in range(1, chips)
    }

    acts = []
    for d in range(chips):
        same = hidden_act
        if d > 0:
            same = lax.ppermute(hidden_act, "col", ahead[d])
        acts += [same, lax.ppermute(same, "col", other_core)]

    edges = [features * sum(EIGHTHS[:p]) // 8 for p in range(len(EIGHTHS) + 1)]
    grads = [ring_gather(out_grad[:, a:b], row_size) for a, b in zip(edges, edges[1:])]

    examples = ring_rows(row_size)
    col = lax.axis_index("col").astype(jnp.uint32)
    owner = examples // per_col
    core = (owner ^ col) & 1
    behind = (col // 2 + chips - owner // 2) % chips
    at = ((behind * 2 + core) * per_col + examples % per_col).astype(jnp.int32)
    before = (owner // 2 + 2 * chips - 1 - col // 2) % chips
    to = ((before * 2 + 1 - core) * per_col + examples % per_col).astype(jnp.int32)

    rows = ()
    for d in range(chips):
        rows = (turned(acts[2 * d : 2 * d + 2], rows, 2 * d * per_col),)
    shape = (units, features)
    blocks = units // row_block(units)
    cuts = [blocks * n // SPLITS for n in range(SPLITS + 1)]
    fisher, sums = None, []
    for p, start in enumerate(edges[:-1]):
        sums = hidden_part(to, grads[p], down_weight, sums, 2 * chips, start)
        for a, b in zip(cuts, cuts[1:]):
            fisher = fisher_part(at, rows[0], grads[p], fisher, shape, a, b - a, start)
    codes = []
    for d in range(1, chips):
        given = lax.ppermute(sums[2 * d - 2], "col", other_core)
        code = by_rows(encode_kernel, units + LANES, jnp.bfloat16, sums[2 * d - 1], given)
        codes.append(lax.ppermute(code, "col", ahead[d]))
    given = lax.ppermute(sums[-2], "col", other_core)
    return fisher, by_rows(decode_kernel, units, jnp.bfloat16, sums[-1], given, *codes)


def whole_kernel(act_ref, grad_ref, out_ref, rows_ref, *, width):
    for e in range(EXAMPLES):
        rows_ref[e, :, :SEQ] = act_ref[e * SEQ : (e + 1) * SEQ, :].T
    for j in range(0, out_ref.shape[1], width):
        total = None
        for e in range(EXAMPLES):
            grad_e = lax.dot_general(
                rows_ref[e, :, :SEQ],
                grad_ref[e * SEQ : (e + 1) * SEQ, j : j + width],
                ROWS_BY_COLUMNS,
                preferred_element_type=F32,
            )
            total = grad_e * grad_e if total is None else total + grad_e * grad_e
        out_ref[:, j : j + width] = total * (1.0 / (EXAMPLES * SEQ))


def gathered(hidden_act, out_grad, down_weight):
    grad = lax.all_gather(out_grad, "row", axis=0, tiled=True)
    act = lax.all_gather(hidden_act, "col", axis=0, tiled=True)
    part = lax.dot_general(grad, down_weight, ROWS_BY_ROWS, preferred_element_type=F32)
    summed = lax.psum_scatter(part, "col", scatter_dimension=0, tiled=True)
    tokens, rows = act.shape
    columns = grad.shape[1]
    block = largest_block(rows, 256)
    fisher = pl.pallas_call(
        functools.partial(whole_kernel, width=largest_block(columns, 256)),
        out_shape=jax.ShapeDtypeStruct((rows, columns), F32),
        grid=(rows // block,),
        in_specs=[
            pl.BlockSpec((tokens, block), lambda i: (0, i)),
            pl.BlockSpec((tokens, columns), lambda i: (0, 0), pipeline_mode=pl.Buffered(1)),
        ],
        out_specs=pl.BlockSpec((block, columns), lambda i: (i, 0)),
        scratch_shapes=[pltpu.VMEM((EXAMPLES, block, LANES), act.dtype)],
        compiler_params=params(),
        name="fisher",
    )(act, grad)
    return fisher, summed.astype(jnp.bfloat16)


def solution(mesh):
    row_size, col_size = mesh.shape["row"], mesh.shape["col"]
    placed = (P("col", "row"), P("row", "col"), P("row", "col"))

    def on_mesh(per_device):
        return jax.shard_map(
            per_device,
            mesh=mesh,
            in_specs=placed,
            out_specs=(P("row", "col"), P("col", "row")),
            check_vma=False,
        )

    def per_device(hidden_act, out_grad, down_weight):
        return pipelined(hidden_act, out_grad, down_weight, row_size, col_size)

    if row_size != EXAMPLES or col_size != 4:
        return on_mesh(gathered)
    return on_mesh(per_device)
```

```python
import functools

import jax
import jax.numpy as jnp
import numpy as np
from jax import lax
from jax.experimental import pallas as pl
from jax.experimental.pallas import tpu as pltpu
from jax.sharding import PartitionSpec as P


SEQ = 96
EXAMPLES = 8
LANES = 128
EIGHTHS = (3, 5)
CUTS = ((0, 2, 5, 8), (0, 2, 8))
BUFFERS = 3
GROUP = 16
HALVED = 1
POWER_TOP = 2.0**7.75

F32 = jnp.float32
ROWS_BY_ROWS = (((1,), (1,)), ((), ()))
ROWS_BY_COLUMNS = (((1,), (0,)), ((), ()))


def largest_block(size, limit):
    return max(b for b in range(LANES, limit + 1, LANES) if size % b == 0)


def params(mib=None):
    limit = {} if mib is None else {"vmem_limit_bytes": mib << 20}
    return pltpu.CompilerParams(dimension_semantics=("arbitrary",), **limit)


def in_vmem():
    return pl.BlockSpec(memory_space=pltpu.VMEM)


def turn_kernel(*refs, slot, step):
    act_refs, rows_ref = refs[:2], refs[-1]
    for act_ref in act_refs:
        for row in range(0, act_ref.shape[0], SEQ):
            for units in range(0, act_ref.shape[1], step):
                rows_ref[slot, units : units + step, :SEQ] = act_ref[
                    row : row + SEQ, units : units + step
                ].T
            slot += 1


def turned(acts, held, slot):
    units = acts[0].shape[1]
    return pl.pallas_call(
        functools.partial(turn_kernel, slot=slot, step=largest_block(units, 256)),
        out_shape=jax.ShapeDtypeStruct((EXAMPLES, units, LANES), acts[0].dtype),
        in_specs=[in_vmem()] * (2 + len(held)),
        out_specs=in_vmem(),
        input_output_aliases={2: 0} if held else {},
        cost_estimate=pl.CostEstimate(
            flops=4 * acts[0].size, bytes_accessed=8 * acts[0].size, transcendentals=0
        ),
        compiler_params=pltpu.CompilerParams(vmem_limit_bytes=16 << 20),
    )(*acts, *held)


def columns_of(refs, slot, start, width):
    if slot < EXAMPLES - 1:
        return refs[slot].at[:, start : start + width]
    held = refs[-1].shape[1]
    return refs[slot + start // held].at[:, start % held : start % held + width]


def fisher_kernel(at_ref, rows_ref, *refs, arrays, width, part, block, first, blocks, start):
    grad_refs = refs[:arrays]
    fisher_ref, out_ref, sems = refs[-3:]
    parts = grad_refs[0].shape[1] // part

    def units(i):
        return pl.ds(pl.multiple_of((first + i) * block, block), block)

    def sending(i, n):
        return pltpu.make_async_copy(
            out_ref.at[n], fisher_ref.at[units(i), pl.ds(start + n * part, part)], sems.at[n]
        )

    def one_block(i, carry):
        for n in range(parts):

            @pl.when(i > 0)
            def _():
                sending(i - 1, n).wait()

            for j in range(0, part, width):
                total = None
                for s in range(EXAMPLES):
                    grad_e = lax.dot_general(
                        rows_ref[at_ref[s], units(i), :SEQ],
                        columns_of(grad_refs, s, n * part + j, width)[...],
                        ROWS_BY_COLUMNS,
                        preferred_element_type=F32,
                    )
                    total = grad_e * grad_e if total is None else total + grad_e * grad_e
                out_ref[n, :, j : j + width] = total * (1.0 / (EXAMPLES * SEQ))
            sending(i, n).start()
        return carry

    lax.fori_loop(0, blocks, one_block, 0)
    for n in range(parts):
        sending(blocks - 1, n).wait()


def row_block(units):
    return max(b for b in range(16, 417, 16) if units % b == 0)


def fisher_part(at, rows, grads, held, shape, first, blocks, start):
    block = row_block(shape[0])
    columns = grads[0].shape[1]
    part = largest_block(columns, columns // 2)
    in_specs = [pl.BlockSpec(memory_space=pltpu.SMEM)] + [in_vmem()] * (1 + len(grads))
    operands = [at, rows, *grads]
    aliases = {}
    if held is not None:
        aliases = {len(operands): 0}
        operands.append(held)
        in_specs.append(pl.BlockSpec(memory_space=pl.ANY))
    tokens = EXAMPLES * SEQ
    return pl.pallas_call(
        functools.partial(
            fisher_kernel,
            arrays=len(grads),
            width=largest_block(part, 256),
            part=part,
            block=block,
            first=first,
            blocks=blocks,
            start=start,
        ),
        out_shape=jax.ShapeDtypeStruct(shape, F32),
        in_specs=in_specs,
        out_specs=pl.BlockSpec(memory_space=pl.ANY),
        scratch_shapes=[
            pltpu.VMEM((columns // part, block, part), F32),
            pltpu.SemaphoreType.DMA((columns // part,)),
        ],
        input_output_aliases=aliases,
        cost_estimate=pl.CostEstimate(
            flops=5 * tokens * blocks * block * columns,
            bytes_accessed=4 * blocks * block * columns,
            transcendentals=0,
        ),
        compiler_params=pltpu.CompilerParams(vmem_limit_bytes=16 << 20),
    )(*operands)


def hidden_kernel(to_ref, *refs, arrays, places, start):
    grad_refs, weight_ref = refs[:arrays], refs[arrays]
    held_refs, out_refs = refs[arrays + 1 : -5 - places], refs[-5 - places : -5]
    tokens_ref, buffer_ref, tail_ref, sems, tail_sem = refs[-5:]
    columns = tokens_ref.shape[2]
    buffers, block = buffer_ref.shape[:2]
    blocks, tail = weight_ref.shape[0] // block, weight_ref.shape[0] % block

    def units(i):
        return pl.ds(pl.multiple_of(i * block, block), block)

    def fetching(i):
        slot = lax.rem(i, buffers)
        return pltpu.make_async_copy(
            weight_ref.at[units(i), pl.ds(start, columns)], buffer_ref.at[slot], sems.at[slot]
        )

    last = pl.ds(blocks * block, tail)
    fetching_tail = pltpu.make_async_copy(
        weight_ref.at[last, pl.ds(start, columns)], tail_ref.at[pl.ds(0, tail)], tail_sem
    )

    for i in range(min(buffers - 1, blocks)):
        fetching(jnp.int32(i)).start()
    if tail:
        fetching_tail.start()
    held = grad_refs[-1].shape[1]
    for s in range(EXAMPLES):
        for column in range(0, columns, held):
            here = slice(column, column + held)
            tokens_ref[to_ref[s], :, here] = columns_of(grad_refs, s, column, held)[...]

    def multiplied(weights, here):
        tokens = tokens_ref[...].reshape(EXAMPLES * SEQ, columns)
        part = lax.dot_general(tokens, weights, ROWS_BY_ROWS, preferred_element_type=F32)
        rows = part.shape[0] // places
        for n, out_ref in enumerate(out_refs):
            piece = part[n * rows : (n + 1) * rows]
            out_ref[:, here] = piece + held_refs[n][:, here] if held_refs else piece

    def one_block(i, carry):
        @pl.when(i + buffers - 1 < blocks)
        def _():
            fetching(i + buffers - 1).start()

        fetching(i).wait()
        multiplied(buffer_ref[lax.rem(i, buffers)], units(i))
        return carry

    lax.fori_loop(0, blocks, one_block, 0)
    if tail:
        fetching_tail.wait()
        multiplied(tail_ref[:tail], last)


def hidden_part(to, grads, weight, held, places, start):
    units = weight.shape[0]
    columns = grads[0].shape[1]
    block = 2 * largest_block(units, 256)
    rows = EXAMPLES * SEQ // places
    return pl.pallas_call(
        functools.partial(hidden_kernel, arrays=len(grads), places=places, start=start),
        out_shape=[jax.ShapeDtypeStruct((rows, units), F32)] * places,
        in_specs=[pl.BlockSpec(memory_space=pltpu.SMEM)]
        + [in_vmem()] * len(grads)
        + [pl.BlockSpec(memory_space=pl.ANY)]
        + [in_vmem()] * len(held),
        out_specs=[in_vmem()] * places,
        scratch_shapes=[
            pltpu.VMEM((EXAMPLES, SEQ, columns), weight.dtype),
            pltpu.VMEM((BUFFERS, block, columns), weight.dtype),
            pltpu.VMEM((units % block or LANES, columns), weight.dtype),
            pltpu.SemaphoreType.DMA((BUFFERS,)),
            pltpu.SemaphoreType.DMA(()),
        ],
        input_output_aliases={2 + len(grads) + n: n for n in range(len(held))},
        cost_estimate=pl.CostEstimate(
            flops=2 * EXAMPLES * SEQ * units * columns,
            bytes_accessed=2 * units * columns,
            transcendentals=0,
        ),
        compiler_params=pltpu.CompilerParams(vmem_limit_bytes=22 << 20),
    )(to, *grads, weight, *held)


def encode_kernel(a_ref, b_ref, code_ref):
    total = a_ref[...] + b_ref[...]
    units = total.shape[1]
    top = jnp.maximum(jnp.max(jnp.abs(total), axis=1, keepdims=True), 1e-35) * 1.004
    scale = jnp.broadcast_to(top, (total.shape[0], LANES)).astype(code_ref.dtype)
    code_ref[:, units:] = scale
    share = total * (POWER_TOP / scale.astype(F32)[:, :1])
    power = share * share
    power = power * power
    power = power * power
    power = power * power
    code_ref[:, :units] = jnp.where(share < 0, -power, power).astype(code_ref.dtype)


def encoded(a, b):
    rows, units = a.shape
    block = 48 if rows % 48 == 0 else rows
    return pl.pallas_call(
        encode_kernel,
        out_shape=jax.ShapeDtypeStruct((rows, units + LANES), jnp.bfloat16),
        grid=(rows // block,),
        in_specs=[pl.BlockSpec((block, units), lambda i: (i, 0))] * 2,
        out_specs=pl.BlockSpec((block, units + LANES), lambda i: (i, 0)),
        cost_estimate=pl.CostEstimate(
            flops=10 * rows * units, bytes_accessed=10 * rows * units, transcendentals=0
        ),
        compiler_params=params(20),
        name="encode",
    )(a, b)


def decode_kernel(*refs):
    mine_ref, other_ref, code_refs = refs[0], refs[1], refs[2:-3]
    result_ref, out_ref, sems = refs[-3:]
    units = mine_ref.shape[1]
    share = mine_ref.shape[0] // sems.shape[0]

    def some_rows(i, carry):
        rows = pl.ds(pl.multiple_of(i * GROUP, GROUP), GROUP)
        total = mine_ref[rows, :] + other_ref[rows, :]
        for code_ref in code_refs:
            power = code_ref[rows, :units].astype(F32)
            root = jnp.exp(jnp.log(jnp.abs(power)) * (1.0 / 16))
            scale = code_ref[rows, units:].astype(F32)[:, :1] * (1.0 / POWER_TOP)
            total = total + jnp.where(power < 0, -root, root) * scale
        out_ref[rows, :] = total.astype(out_ref.dtype)
        return carry

    def sending(n):
        rows = pl.ds(n * share, share)
        return pltpu.make_async_copy(out_ref.at[rows], result_ref.at[rows], sems.at[n])

    for n in range(sems.shape[0]):
        lax.fori_loop(n * share // GROUP, (n + 1) * share // GROUP, some_rows, 0)
        sending(n).start()
    for n in range(sems.shape[0]):
        sending(n).wait()


def decoded(mine, other, codes):
    rows, units = mine.shape
    shares = 4 if rows % (4 * GROUP) == 0 else 1
    return pl.pallas_call(
        decode_kernel,
        out_shape=jax.ShapeDtypeStruct((rows, units), jnp.bfloat16),
        in_specs=[in_vmem()] * (2 + len(codes)),
        out_specs=pl.BlockSpec(memory_space=pl.ANY),
        scratch_shapes=[
            pltpu.VMEM((rows, units), jnp.bfloat16),
            pltpu.SemaphoreType.DMA((shares,)),
        ],
        cost_estimate=pl.CostEstimate(
            flops=10 * rows * units, bytes_accessed=10 * rows * units, transcendentals=0
        ),
        compiler_params=pltpu.CompilerParams(vmem_limit_bytes=8 << 20),
        name="decode",
    )(mine, other, *codes)


def ring_places(size):
    return list(range(0, size, 2)) + list(range(size - 1, 0, -2))


def ring_gather(piece, size, halved):
    ring = ring_places(size)
    right = [(ring[n], ring[(n + 1) % size]) for n in range(size)]
    left = [(b, a) for a, b in right]
    found, from_left, from_right = [piece], piece, piece
    last, half = size // 2, piece.shape[1] // 2
    for _ in range(1, last):
        from_left = lax.ppermute(from_left, "row", right)
        from_right = lax.ppermute(from_right, "row", left)
        found += [from_left, from_right]
    if not halved:
        return found + [lax.ppermute(from_left, "row", right)]
    found.append(lax.ppermute(from_left[:, :half], "row", right))
    found.append(lax.ppermute(from_right[:, half:], "row", left))
    return found


def ring_rows(size):
    steps = [0]
    for step in range(1, size // 2 + 1):
        steps.append(size - step)
        if step < size - size // 2:
            steps.append(step)
    row = lax.axis_index("row").astype(jnp.uint32)
    mine = jnp.where(row % 2 == 0, row // 2, size - 1 - row // 2)
    places = (mine + np.array(steps, np.uint32)) % size
    return jnp.where(places < size // 2, 2 * places, 2 * (size - 1 - places) + 1)


def pipelined(hidden_act, out_grad, down_weight, row_size, col_size):
    chips = col_size // 2
    units, features = down_weight.shape
    per_col = hidden_act.shape[0] // SEQ
    other_core = [(c, c ^ 1) for c in range(col_size)]
    ahead = {
        d: [(c, (c + 2 * d) % col_size) for c in range(col_size)] for d in range(1, chips)
    }

    acts = []
    for d in range(chips):
        same = hidden_act
        if d > 0:
            same = lax.ppermute(hidden_act, "col", ahead[d])
        acts += [same, lax.ppermute(same, "col", other_core)]

    edges = [features * sum(EIGHTHS[:p]) // 8 for p in range(len(EIGHTHS) + 1)]
    grads = [
        ring_gather(out_grad[:, a:b], row_size, p < HALVED)
        for p, (a, b) in enumerate(zip(edges, edges[1:]))
    ]

    examples = ring_rows(row_size)
    col = lax.axis_index("col").astype(jnp.uint32)
    owner = examples // per_col
    core = (owner ^ col) & 1
    behind = (col // 2 + chips - owner // 2) % chips
    at = ((behind * 2 + core) * per_col + examples % per_col).astype(jnp.int32)
    before = (owner // 2 + 2 * chips - 1 - col // 2) % chips
    to = ((before * 2 + 1 - core) * per_col + examples % per_col).astype(jnp.int32)

    rows = ()
    for d in range(chips):
        rows = (turned(acts[2 * d : 2 * d + 2], rows, 2 * d * per_col),)
    shape = (units, features)
    blocks = units // row_block(units)
    fisher, sums = None, []
    for p, start in enumerate(edges[:-1]):
        sums = hidden_part(to, grads[p], down_weight, sums, 2 * chips, start)
        cuts = [blocks * eighths // 8 for eighths in CUTS[p]]
        for a, b in zip(cuts, cuts[1:]):
            fisher = fisher_part(at, rows[0], grads[p], fisher, shape, a, b - a, start)
    codes = []
    for d in range(1, chips):
        given = lax.ppermute(sums[2 * d - 2], "col", other_core)
        code = encoded(sums[2 * d - 1], given)
        codes.append(lax.ppermute(code, "col", ahead[d]))
    given = lax.ppermute(sums[-2], "col", other_core)
    return fisher, decoded(sums[-1], given, codes)


def whole_kernel(act_ref, grad_ref, out_ref, rows_ref, *, width):
    for e in range(EXAMPLES):
        rows_ref[e, :, :SEQ] = act_ref[e * SEQ : (e + 1) * SEQ, :].T
    for j in range(0, out_ref.shape[1], width):
        total = None
        for e in range(EXAMPLES):
            grad_e = lax.dot_general(
                rows_ref[e, :, :SEQ],
                grad_ref[e * SEQ : (e + 1) * SEQ, j : j + width],
                ROWS_BY_COLUMNS,
                preferred_element_type=F32,
            )
            total = grad_e * grad_e if total is None else total + grad_e * grad_e
        out_ref[:, j : j + width] = total * (1.0 / (EXAMPLES * SEQ))


def gathered(hidden_act, out_grad, down_weight):
    grad = lax.all_gather(out_grad, "row", axis=0, tiled=True)
    act = lax.all_gather(hidden_act, "col", axis=0, tiled=True)
    part = lax.dot_general(grad, down_weight, ROWS_BY_ROWS, preferred_element_type=F32)
    summed = lax.psum_scatter(part, "col", scatter_dimension=0, tiled=True)
    tokens, rows = act.shape
    columns = grad.shape[1]
    block = largest_block(rows, 256)
    fisher = pl.pallas_call(
        functools.partial(whole_kernel, width=largest_block(columns, 256)),
        out_shape=jax.ShapeDtypeStruct((rows, columns), F32),
        grid=(rows // block,),
        in_specs=[
            pl.BlockSpec((tokens, block), lambda i: (0, i)),
            pl.BlockSpec((tokens, columns), lambda i: (0, 0), pipeline_mode=pl.Buffered(1)),
        ],
        out_specs=pl.BlockSpec((block, columns), lambda i: (i, 0)),
        scratch_shapes=[pltpu.VMEM((EXAMPLES, block, LANES), act.dtype)],
        compiler_params=params(),
        name="fisher",
    )(act, grad)
    return fisher, summed.astype(jnp.bfloat16)


def solution(mesh):
    row_size, col_size = mesh.shape["row"], mesh.shape["col"]
    placed = (P("col", "row"), P("row", "col"), P("row", "col"))

    def on_mesh(per_device):
        return jax.shard_map(
            per_device,
            mesh=mesh,
            in_specs=placed,
            out_specs=(P("row", "col"), P("col", "row")),
            check_vma=False,
        )

    def per_device(hidden_act, out_grad, down_weight):
        return pipelined(hidden_act, out_grad, down_weight, row_size, col_size)

    if row_size != EXAMPLES or col_size != 4:
        return on_mesh(gathered)
    return on_mesh(per_device)
```
